128 devices in a mesh: row: 16 (over y, z), col: 8 (over x, core).
Axes of the slice: x: 4, y: 4, z: 4, core: 2. Of those that a mesh axis runs over, the one named last changes fastest.
Arguments:
- saved_inputs: bfloat16 [32768, 4096], P(('row', 'col')), may hold values from -6 to 6
- output_grads: bfloat16 [32768, 14336], P(('row', 'col')), may hold values from -0.5 to 0.5
- proj_in: bfloat16 [4096, 128], replicated, may hold values from -0.09375 to 0.09375
- proj_out: bfloat16 [14336, 128], replicated, may hold values from -0.046875 to 0.046875
- doc_lengths: int32 [128], replicated, may hold values from 64 to 448, as said below
- device_docs: int32 [128], replicated, may hold values from 0 to 127, as said below
- fisher_inverse: float32 [16384, 16384], P('row', 'col'), may hold values from -0.3 to 2.3, as said below
Outputs:
- preconditioned: float32 [128, 16384], P('row', 'col')
The draws below stay inside these ranges and needn't reach their ends.
Inputs may be any that keep to these rules, and one draw needn't show every extreme that they name: `doc_lengths`: the lengths sum to 32768; some document has exactly 448 tokens and some exactly 64. `device_docs`: A permutation of the documents. `fisher_inverse`: Symmetric.
All inputs are finite; a program needn't handle non-finite values.
Results may differ from the reference program's by a relative error of at most 0.0041.
Values sent between devices are 32-bit elements; how exact they have to be, the bound alone decides.
A program may use at most 128 MiB of HBM per device.

```python
import math
import jax
import jax.numpy as jnp
from jax import lax

D = 4096
FF = 14336
RANK_IN = 128
RANK_OUT = 128
TOK_DEV = 256
NFEAT = 16384
TOKENS = 32768
NDOC = 128
MEANLEN = 256
SPREAD = 192
MINLEN = 64


def draw_doc_lengths(key, part):
    key_extra, key_pick = jax.random.split(jax.random.fold_in(key, 11))
    extra = jax.random.randint(key_extra, (NDOC,), 0, SPREAD + 1)
    start_doc = jax.random.randint(key_pick, (), 1, NDOC - 8)
    index = jnp.arange(NDOC)
    fixed_points = (index == 0) | (index == start_doc - 1) | (index == start_doc + 9)
    extra = jnp.where(fixed_points, 0, extra)
    lengths = MEANLEN + extra - jnp.roll(extra, -1)
    planted = jnp.array([MINLEN, SPREAD + 1, MINLEN, MINLEN, MINLEN, MEANLEN + SPREAD, MEANLEN + SPREAD, MEANLEN + SPREAD, MEANLEN + SPREAD, MEANLEN + MINLEN - 1], dtype=jnp.int32)
    offset = index - (start_doc - 1)
    inside = (offset >= 0) & (offset < 10)
    lengths = jnp.where(inside, planted[jnp.clip(offset, 0, 9)], lengths)
    return lengths.astype(jnp.int32)


def draw_device_docs(key, part):
    first = jax.random.randint(jax.random.fold_in(key, 31), (), 0, NDOC)
    second = (first + 1) % NDOC
    third = (first + 1 + NDOC // 2) % NDOC
    index = jnp.arange(NDOC, dtype=jnp.int32)
    owners = jnp.where(index == first, second, jnp.where(index == second, third, jnp.where(index == third, first, index)))
    return owners.astype(jnp.int32)


def draw_fisher_inverse(key, part):
    key_noise, key_diag = jax.random.split(jax.random.fold_in(key, 23))
    noise = jnp.clip(jax.random.normal(key_noise, (NFEAT, NFEAT), jnp.float32), -4.0, 4.0)
    off_diag = 0.5 * (noise + noise.T) / math.sqrt(2.0 * NFEAT)
    diag_vals = jnp.exp(jax.random.uniform(key_diag, (NFEAT,), jnp.float32, math.log(0.5), math.log(2.0)))
    return (off_diag + jnp.diag(diag_vals)).astype(jnp.float32)


def level_of(key, dims, cuts, least, largest):
    def one(axis_at, parts):
        draws = jax.random.uniform(jax.random.fold_in(jax.random.fold_in(key, 6), axis_at), (parts,), jnp.float32, least / len(cuts), largest / len(cuts))
        return jnp.repeat(jnp.exp(draws), dims[axis_at] // parts).reshape((-1,) + (1,) * (len(dims) - axis_at - 1))

    gain = one(*cuts[0])
    for cut in cuts[1:]:
        gain = gain * one(*cut)
    return gain


def bell_draw(stream_key, dims, width, bound, cuts=(), held_as=jnp.bfloat16):
    drawn = width * jax.random.normal(stream_key, dims, jnp.float32)
    if cuts:
        drawn = drawn * level_of(stream_key, dims, cuts, -0.22, 0.18)
    return jnp.clip(drawn, -bound, bound).astype(held_as)


def setup_inputs(seed: int = 0) -> dict:
    key_list = jax.random.split(jax.random.key(seed), 8)
    return {
        "saved_inputs": bell_draw(key_list[0], (TOKENS, D), 1.0, 6.0, ((0, 128),)),
        "output_grads": bell_draw(key_list[1], (TOKENS, FF), 0.0625, 0.5, ((0, 128),)),
        "proj_in": bell_draw(key_list[2], (D, RANK_IN), D ** -0.5, 0.09375),
        "proj_out": bell_draw(key_list[3], (FF, RANK_OUT), FF ** -0.5, 0.046875),
        "doc_lengths": draw_doc_lengths(jax.random.fold_in(key_list[7], 71), 0),
        "device_docs": draw_device_docs(jax.random.fold_in(key_list[7], 71), 0),
        "fisher_inverse": draw_fisher_inverse(jax.random.fold_in(key_list[7], 71), 0),
    }


def reference(saved_inputs, output_grads, proj_in, proj_out, doc_lengths, device_docs, fisher_inverse):
    low_in = jnp.dot(saved_inputs, proj_in, preferred_element_type=jnp.float32).astype(jnp.bfloat16)
    low_out = jnp.dot(output_grads, proj_out, preferred_element_type=jnp.float32).astype(jnp.bfloat16)
    doc_ends = jnp.cumsum(doc_lengths)
    starts = doc_ends - doc_lengths
    positions = jnp.arange(TOKENS, dtype=jnp.int32)
    doc_ids = jnp.sum((starts[None, :] <= positions[:, None]).astype(jnp.int32), axis=1) - 1
    block_count = TOKENS // TOK_DEV
    ids_blocks = doc_ids.reshape(block_count, TOK_DEV)
    in_blocks = low_in.reshape(block_count, TOK_DEV, RANK_IN)
    out_blocks = low_out.reshape(block_count, TOK_DEV, RANK_OUT)
    doc_range = jnp.arange(NDOC, dtype=jnp.int32)

    def accumulate(total, pieces):
        block_ids, rows_in, rows_out = pieces
        onehot = (block_ids[:, None] == doc_range[None, :]).astype(rows_out.dtype)
        masked = (onehot[:, :, None] * rows_out[:, None, :]).reshape(TOK_DEV, NDOC * RANK_OUT)
        term = lax.dot_general(masked, rows_in, (((0,), (0,)), ((), ())), preferred_element_type=jnp.float32)
        return total + term, None

    start_total = jnp.zeros((NDOC * RANK_OUT, RANK_IN), jnp.float32)
    total, _ = lax.scan(accumulate, start_total, (ids_blocks, in_blocks, out_blocks))
    grads = total.reshape(NDOC, NFEAT)
    owned = grads[device_docs.astype(jnp.int32)]
    return jnp.dot(owned, fisher_inverse, precision=lax.Precision.HIGHEST, preferred_element_type=jnp.float32)
```

```python
import jax
import jax.numpy as jnp
from jax import lax
from jax.experimental import pallas as pl
from jax.experimental.pallas import tpu as pltpu
from jax.sharding import PartitionSpec as P

SLOTS = 5
F32 = jnp.float32
BF16 = jnp.bfloat16
MESH = pl.DeviceIdType.MESH


def split(x):
    hi = x.astype(BF16)
    return hi, (x - hi.astype(F32)).astype(BF16)


def dot(a, b):
    return jnp.dot(a, b, preferred_element_type=F32)


def body(
    chunk, si, og, pi, po, dl, dd, fi, out,
    x, w, f32buf, fhi, flo, sel, pbuf, rbuf, sbuf, tbuf, gbuf, ybuf, obuf,
    x_sem, w_sem, f_sem, s1, r1, s2, r2, s3, r3, s4, r4,
):
    n_row = lax.axis_size("row")
    n_col = lax.axis_size("col")
    row = lax.axis_index("row")
    col = lax.axis_index("col")
    tok, d_in = si.shape
    rank = pi.shape[1]
    docs = dl.shape[1]
    n_in = d_in // chunk
    n_all = n_in + og.shape[1] // chunk
    piece = SLOTS * n_col
    lot = SLOTS * n_row

    loads = []
    for k in range(n_all):
        a, b, i = (si, pi, k) if k < n_in else (og, po, k - n_in)
        cols = pl.ds(i * chunk, chunk)
        loads.append((
            pltpu.make_async_copy(a.at[:, cols], x.at[k], x_sem.at[k]),
            pltpu.make_async_copy(b.at[cols, :], w.at[k], w_sem.at[k]),
        ))
        for c in loads[-1]:
            c.start()
    f_load = pltpu.make_async_copy(fi, f32buf, f_sem)
    f_load.start()

    barrier = pltpu.get_barrier_semaphore()

    @pl.loop(1, n_row)
    def _(j):
        pl.semaphore_signal(barrier, inc=1, device_id={"row": lax.rem(row + j, n_row), "col": col}, device_id_type=MESH)

    @pl.loop(1, n_col)
    def _(j):
        pl.semaphore_signal(barrier, inc=1, device_id={"row": row, "col": lax.rem(col + j, n_col)}, device_id_type=MESH)

    lens = jnp.broadcast_to(dl[...].astype(F32), (docs, docs))
    down = lax.broadcasted_iota(jnp.int32, (docs, docs), 0)
    along = lax.broadcasted_iota(jnp.int32, (docs, docs), 1)
    starts_col = jnp.sum(jnp.where(along < down, lens, 0.0), axis=1, keepdims=True)
    starts_row = jnp.sum(jnp.where(down == along, starts_col, 0.0), axis=0, keepdims=True)
    owner_col = jnp.sum(jnp.where(down == along, dd[...].astype(F32), 0.0), axis=1, keepdims=True)

    lanes = lax.broadcasted_iota(jnp.int32, (1, n_col * lot), 1)
    shard = lax.rem(lanes, lot) // SLOTS * n_col + lanes // lot
    first = jnp.sum(jnp.where(starts_col <= (shard * tok).astype(F32), 1.0, 0.0), axis=0, keepdims=True) - 1.0
    slot_doc = first + lax.rem(lanes, SLOTS).astype(F32)
    sel[...] = jnp.where(owner_col == slot_doc, 1.0, 0.0).astype(BF16)

    base = (row * n_col + col) * tok
    pos = base + lax.broadcasted_iota(jnp.int32, (tok, 1), 0)
    begun = (starts_row <= pos.astype(F32)) & (starts_row > jnp.full((1, 1), base, jnp.int32).astype(F32))
    slot = jnp.sum(jnp.where(begun, 1.0, 0.0), axis=1, keepdims=True)

    low = []
    for lo, hi in ((0, n_in), (n_in, n_all)):
        acc = None
        for k in range(lo, hi):
            for c in loads[k]:
                c.wait()
            term = dot(x[k], w[k])
            acc = term if acc is None else acc + term
        low.append(acc.astype(BF16))
    low_in, low_out = low
    masked = jnp.concatenate(
        [jnp.where(slot == float(s), low_in, jnp.zeros_like(low_in)) for s in range(SLOTS)], axis=1
    )
    part = lax.dot_general(low_out, masked, (((0,), (0,)), ((), ())), preferred_element_type=F32)
    for r in range(n_row):
        for s in range(SLOTS):
            pbuf[pl.ds(r * piece + s * n_col, n_col), :] = part[r * n_col:(r + 1) * n_col, s * rank:(s + 1) * rank]

    pl.semaphore_wait(barrier, n_row + n_col - 2)

    def over_row(src, dst, send, recv, j, step):
        to = lax.rem(row + j, n_row)
        return pltpu.make_async_remote_copy(
            src_ref=src.at[pl.ds(to * step, step), :], dst_ref=dst.at[pl.ds(row * step, step), :],
            send_sem=send.at[j], recv_sem=recv.at[j], device_id={"row": to, "col": col}, device_id_type=MESH,
        )

    def over_col(src, dst, send, recv, j, step, whole):
        to = lax.rem(col + j, n_col)
        at = col if whole else to
        return pltpu.make_async_remote_copy(
            src_ref=src.at[pl.ds(at * step, step), :], dst_ref=dst.at[pl.ds(col * step, step), :],
            send_sem=send.at[j], recv_sem=recv.at[j], device_id={"row": row, "col": to}, device_id_type=MESH,
        )

    @pl.loop(1, n_row)
    def _(j):
        over_row(pbuf, rbuf, s1, r1, j, piece).start()

    rbuf[pl.ds(row * piece, piece), :] = pbuf[pl.ds(row * piece, piece), :]

    f_load.wait()

    @pl.loop(0, fi.shape[0] // 32)
    def _(i):
        at = pl.ds(pl.multiple_of(i * 32, 32), 32)
        fhi[at, :], flo[at, :] = split(f32buf[at, :])

    @pl.loop(1, n_row)
    def _(j):
        over_row(pbuf, rbuf, s1, r1, j, piece).wait()

    for c in range(n_col):
        sbuf[pl.ds(c * lot, lot), :] = rbuf[pl.ds(c, lot, stride=n_col), :]

    @pl.loop(1, n_col)
    def _(j):
        over_col(sbuf, tbuf, s2, r2, j, lot, False).start()

    tbuf[pl.ds(col * lot, lot), :] = sbuf[pl.ds(col * lot, lot), :]

    @pl.loop(1, n_col)
    def _(j):
        over_col(sbuf, tbuf, s2, r2, j, lot, False).wait()

    t_hi, t_lo = split(tbuf[...])
    gbuf[pl.ds(col * docs, docs), :] = dot(sel[...], t_hi) + dot(sel[...], t_lo)

    @pl.loop(1, n_col)
    def _(j):
        over_col(gbuf, gbuf, s3, r3, j, docs, True).start()

    @pl.loop(1, n_col)
    def _(j):
        over_col(gbuf, gbuf, s3, r3, j, docs, True).wait()

    g = jnp.concatenate([gbuf[c * docs:(c + 1) * docs, :] for c in range(n_col)], axis=1)
    g_hi, g_lo = split(g)

    @pl.loop(0, ybuf.shape[1] // 256)
    def _(n):
        at = pl.ds(pl.multiple_of(n * 256, 256), 256)
        ybuf[:, at] = dot(g_hi, fhi[:, at]) + (dot(g_hi, flo[:, at]) + dot(g_lo, fhi[:, at]))

    rows = docs // n_row

    @pl.loop(1, n_row)
    def _(j):
        over_row(ybuf, obuf, s4, r4, j, rows).start()

    obuf[pl.ds(row * rows, rows), :] = ybuf[pl.ds(row * rows, rows), :]

    @pl.loop(1, n_row)
    def _(j):
        over_row(ybuf, obuf, s4, r4, j, rows).wait()

    total = obuf[0:rows, :]
    for r in range(1, n_row):
        total = total + obuf[r * rows:(r + 1) * rows, :]
    out[...] = total


def per_device(saved_inputs, output_grads, proj_in, proj_out, doc_lengths, device_docs, fisher_inverse):
    n_row, n_col = lax.axis_size("row"), lax.axis_size("col")
    tok, d_in = saved_inputs.shape
    ff = output_grads.shape[1]
    rank = proj_in.shape[1]
    docs = doc_lengths.shape[0]
    feats, cols = fisher_inverse.shape
    chunk = 2048
    n_all = (d_in + ff) // chunk
    slots = n_row * n_col * SLOTS
    dma = pltpu.SemaphoreType.DMA
    hbm = pl.BlockSpec(memory_space=pl.ANY)
    vmem = pl.BlockSpec(memory_space=pltpu.VMEM)

    def kernel(*refs):
        body(chunk, *refs)

    return pl.pallas_call(
        kernel,
        out_shape=jax.ShapeDtypeStruct((docs // n_row, cols), F32),
        in_specs=[hbm, hbm, hbm, hbm, vmem, vmem, hbm],
        out_specs=vmem,
        scratch_shapes=[
            pltpu.VMEM((n_all, tok, chunk), BF16),
            pltpu.VMEM((n_all, chunk, rank), BF16),
            pltpu.VMEM((feats, cols), F32),
            pltpu.VMEM((feats, cols), BF16),
            pltpu.VMEM((feats, cols), BF16),
            pltpu.VMEM((docs, slots), BF16),
            pltpu.VMEM((slots, rank), F32),
            pltpu.VMEM((slots, rank), F32),
            pltpu.VMEM((slots, rank), F32),
            pltpu.VMEM((slots, rank), F32),
            pltpu.VMEM((n_col * docs, rank), F32),
            pltpu.VMEM((docs, cols), F32),
            pltpu.VMEM((docs, cols), F32),
            dma((n_all,)), dma((n_all,)), dma,
            dma((n_row,)), dma((n_row,)), dma((n_col,)), dma((n_col,)),
            dma((n_col,)), dma((n_col,)), dma((n_row,)), dma((n_row,)),
        ],
        compiler_params=pltpu.CompilerParams(
            collective_id=0, has_side_effects=True, vmem_limit_bytes=56 << 20
        ),
    )(
        saved_inputs, output_grads, proj_in, proj_out,
        doc_lengths.reshape(1, docs), device_docs.reshape(1, docs), fisher_inverse,
    )


def solution(mesh):
    placed = (P(("row", "col"), None), P(("row", "col"), None), P(), P(), P(), P(), P("row", "col"))
    return jax.shard_map(
        per_device, mesh=mesh, in_specs=placed, out_specs=P("row", "col"), check_vma=False
    )
```

```python
import jax
import jax.numpy as jnp
from jax import lax
from jax.experimental import pallas as pl
from jax.experimental.pallas import tpu as pltpu
from jax.sharding import PartitionSpec as P

SLOTS = 5
CORES = 2
NZ = 4
CHUNKS = 4
F32 = jnp.float32
BF16 = jnp.bfloat16
MESH = pl.DeviceIdType.MESH


def split(x):
    hi = x.astype(BF16)
    return hi, (x - hi.astype(F32)).astype(BF16)


def dot(a, b):
    return jnp.dot(a, b, preferred_element_type=F32)


def body(
    chunk, si, og, pi, po, dl, dd, fi, out,
    x, w, f32buf, fhi, flo, sel, pbuf, rbuf, sbuf, tbuf, gbuf, ghi, glo, ybuf, mbuf, qbuf, obuf,
    x_sem, w_sem, f_sem, s1, r1, s2, r2, s3, r3, s5, r5, s4, r4, s6, r6,
):
    n_row = lax.axis_size("row")
    n_col = lax.axis_size("col")
    row = lax.axis_index("row")
    col = lax.axis_index("col")
    tok, d_in = si.shape
    rank = pi.shape[1]
    docs = dl.shape[1]
    n_in = d_in // chunk
    n_all = n_in + og.shape[1] // chunk
    piece = SLOTS * n_col
    lot = SLOTS * n_row

    loads = []
    for k in range(n_all):
        a, b, i = (si, pi, k) if k < n_in else (og, po, k - n_in)
        cols = pl.ds(i * chunk, chunk)
        loads.append((
            pltpu.make_async_copy(a.at[:, cols], x.at[k], x_sem.at[k]),
            pltpu.make_async_copy(b.at[cols, :], w.at[k], w_sem.at[k]),
        ))
        for c in loads[-1]:
            c.start()
    f_load = pltpu.make_async_copy(fi, f32buf, f_sem)
    f_load.start()

    barrier = pltpu.get_barrier_semaphore()

    @pl.loop(1, n_row)
    def _(j):
        pl.semaphore_signal(barrier, inc=1, device_id={"row": lax.rem(row + j, n_row), "col": col}, device_id_type=MESH)

    @pl.loop(1, n_col)
    def _(j):
        pl.semaphore_signal(barrier, inc=1, device_id={"row": row, "col": lax.rem(col + j, n_col)}, device_id_type=MESH)

    lens = jnp.broadcast_to(dl[...].astype(F32), (docs, docs))
    down = lax.broadcasted_iota(jnp.int32, (docs, docs), 0)
    along = lax.broadcasted_iota(jnp.int32, (docs, docs), 1)
    starts_col = jnp.sum(jnp.where(along < down, lens, 0.0), axis=1, keepdims=True)
    starts_row = jnp.sum(jnp.where(down == along, starts_col, 0.0), axis=0, keepdims=True)
    owner_col = jnp.sum(jnp.where(down == along, dd[...].astype(F32), 0.0), axis=1, keepdims=True)

    lanes = lax.broadcasted_iota(jnp.int32, (1, n_col * lot), 1)
    shard = lax.rem(lanes, lot) // SLOTS * n_col + lanes // lot
    first = jnp.sum(jnp.where(starts_col <= (shard * tok).astype(F32), 1.0, 0.0), axis=0, keepdims=True) - 1.0
    slot_doc = first + lax.rem(lanes, SLOTS).astype(F32)
    sel[...] = jnp.where(owner_col == slot_doc, 1.0, 0.0).astype(BF16)

    base = (row * n_col + col) * tok
    pos = base + lax.broadcasted_iota(jnp.int32, (tok, 1), 0)
    begun = (starts_row <= pos.astype(F32)) & (starts_row > jnp.full((1, 1), base, jnp.int32).astype(F32))
    slot = jnp.sum(jnp.where(begun, 1.0, 0.0), axis=1, keepdims=True)

    low = []
    for lo, hi in ((0, n_in), (n_in, n_all)):
        acc = None
        for k in range(lo, hi):
            for c in loads[k]:
                c.wait()
            term = dot(x[k], w[k])
            acc = term if acc is None else acc + term
        low.append(acc.astype(BF16))
    low_in, low_out = low
    masked = jnp.concatenate(
        [jnp.where(slot == float(s), low_in, jnp.zeros_like(low_in)) for s in range(SLOTS)], axis=1
    )
    part = lax.dot_general(low_out, masked, (((0,), (0,)), ((), ())), preferred_element_type=F32)
    for r in range(n_row):
        for s in range(SLOTS):
            pbuf[pl.ds(r * piece + s * n_col, n_col), :] = part[r * n_col:(r + 1) * n_col, s * rank:(s + 1) * rank]

    pl.semaphore_wait(barrier, n_row + n_col - 2)

    def over_row(src, dst, send, recv, j, step):
        to = lax.rem(row + j, n_row)
        return pltpu.make_async_remote_copy(
            src_ref=src.at[pl.ds(to * step, step), :], dst_ref=dst.at[pl.ds(row * step, step), :],
            send_sem=send.at[j], recv_sem=recv.at[j], device_id={"row": to, "col": col}, device_id_type=MESH,
        )

    def over_col(src, dst, send, recv, j, step, whole):
        to = lax.rem(col + j, n_col)
        at = col if whole else to
        return pltpu.make_async_remote_copy(
            src_ref=src.at[pl.ds(at * step, step), :], dst_ref=dst.at[pl.ds(col * step, step), :],
            send_sem=send.at[j], recv_sem=recv.at[j], device_id={"row": row, "col": to}, device_id_type=MESH,
        )

    @pl.loop(1, n_row)
    def _(j):
        over_row(pbuf, rbuf, s1, r1, j, piece).start()

    rbuf[pl.ds(row * piece, piece), :] = pbuf[pl.ds(row * piece, piece), :]

    f_load.wait()

    @pl.loop(0, fi.shape[0] // 32)
    def _(i):
        at = pl.ds(pl.multiple_of(i * 32, 32), 32)
        fhi[at, :], flo[at, :] = split(f32buf[at, :])

    @pl.loop(1, n_row)
    def _(j):
        over_row(pbuf, rbuf, s1, r1, j, piece).wait()

    for c in range(n_col):
        sbuf[pl.ds(c * lot, lot), :] = rbuf[pl.ds(c, lot, stride=n_col), :]

    @pl.loop(1, n_col)
    def _(j):
        over_col(sbuf, tbuf, s2, r2, j, lot, False).start()

    tbuf[pl.ds(col * lot, lot), :] = sbuf[pl.ds(col * lot, lot), :]

    @pl.loop(1, n_col)
    def _(j):
        over_col(sbuf, tbuf, s2, r2, j, lot, False).wait()

    t_hi, t_lo = split(tbuf[...])
    gbuf[col] = dot(sel[...], t_hi) + dot(sel[...], t_lo)

    nx = n_col // CORES
    cx = col // CORES
    core = lax.rem(col, CORES)
    sibling = col + 1 - 2 * core

    def hand(at, to, send, recv):
        return pltpu.make_async_remote_copy(
            src_ref=gbuf.at[at], dst_ref=gbuf.at[at], send_sem=send, recv_sem=recv,
            device_id={"row": row, "col": to}, device_id_type=MESH,
        )

    def keep(at):
        ghi[at], glo[at] = split(gbuf[at])

    around = [hand(col, lax.rem(cx + j, nx) * CORES + core, s3.at[j], r3.at[j]) for j in range(1, nx)]
    across = [hand(col, sibling, s5.at[0], r5.at[0])]
    for c in around + across:
        c.start()
    keep(col)
    for j in range(1, nx):
        around[j - 1].wait_recv()
        at = lax.rem(cx + nx - j, nx) * CORES + core
        across.append(hand(at, sibling, s5.at[j], r5.at[j]))
        across[j].start()
        keep(at)
    for j in range(nx):
        across[j].wait_recv()
        keep(lax.rem(cx + nx - j, nx) * CORES + 1 - core)

    ny = n_row // NZ
    y, z = row // NZ, lax.rem(row, NZ)
    rows = docs // n_row
    wide = ybuf.shape[3] // CHUNKS
    g_hi = jnp.concatenate([ghi[c] for c in range(n_col)], axis=1)
    g_lo = jnp.concatenate([glo[c] for c in range(n_col)], axis=1)

    def peer(along_y, j):
        if along_y:
            to = lax.rem(y + j, ny)
            return to, {"row": to * NZ + z, "col": col}
        to = lax.rem(z + j, NZ)
        return to, {"row": y * NZ + to, "col": col}

    first_hop, second_hop = [], []
    for n in range(CHUNKS):
        cols = slice(n * wide, (n + 1) * wide)
        f_hi, f_lo = fhi[:, cols], flo[:, cols]
        prod = dot(g_hi, f_hi) + (dot(g_hi, f_lo) + dot(g_lo, f_hi))
        ybuf[:, :, :, cols] = prod.reshape(ny, NZ, rows, wide)
        hops = []
        for j in range(1, ny if n % 2 == 0 else NZ):
            to, device = peer(n % 2 == 0, j)
            src = ybuf.at[to, :, :, cols] if n % 2 == 0 else ybuf.at[:, to, :, cols]
            hops.append(pltpu.make_async_remote_copy(
                src_ref=src, dst_ref=mbuf.at[n, j - 1], send_sem=s4.at[n, j], recv_sem=r4.at[n, j],
                device_id=device, device_id_type=MESH,
            ))
            hops[-1].start()
        first_hop.append(hops)

    for n in range(CHUNKS):
        cols = slice(n * wide, (n + 1) * wide)
        part = ybuf[y, :, :, cols] if n % 2 == 0 else ybuf[:, z, :, cols]
        for j, c in enumerate(first_hop[n]):
            c.wait_recv()
            part = part + mbuf[n, j]
        qbuf[n] = part
        hops = []
        for j in range(1, NZ if n % 2 == 0 else ny):
            to, device = peer(n % 2 == 1, j)
            hops.append(pltpu.make_async_remote_copy(
                src_ref=qbuf.at[n, to], dst_ref=obuf.at[n, j - 1], send_sem=s6.at[n, j], recv_sem=r6.at[n, j],
                device_id=device, device_id_type=MESH,
            ))
            hops[-1].start()
        second_hop.append(hops)

    for n in range(CHUNKS):
        total = qbuf[n, z if n % 2 == 0 else y]
        for j, c in enumerate(second_hop[n]):
            c.wait_recv()
            total = total + obuf[n, j]
        out[:, n * wide:(n + 1) * wide] = total

    for c in around + across + sum(first_hop + second_hop, []):
        c.wait_send()


def per_device(saved_inputs, output_grads, proj_in, proj_out, doc_lengths, device_docs, fisher_inverse):
    n_row, n_col = lax.axis_size("row"), lax.axis_size("col")
    tok, d_in = saved_inputs.shape
    ff = output_grads.shape[1]
    rank = proj_in.shape[1]
    docs = doc_lengths.shape[0]
    feats, cols = fisher_inverse.shape
    chunk = 2048
    n_all = (d_in + ff) // chunk
    slots = n_row * n_col * SLOTS
    ny, nx, rows = n_row // NZ, n_col // CORES, docs // n_row
    dma = pltpu.SemaphoreType.DMA
    hbm = pl.BlockSpec(memory_space=pl.ANY)
    vmem = pl.BlockSpec(memory_space=pltpu.VMEM)

    def kernel(*refs):
        body(chunk, *refs)

    return pl.pallas_call(
        kernel,
        out_shape=jax.ShapeDtypeStruct((docs // n_row, cols), F32),
        in_specs=[hbm, hbm, hbm, hbm, vmem, vmem, hbm],
        out_specs=vmem,
        scratch_shapes=[
            pltpu.VMEM((n_all, tok, chunk), BF16),
            pltpu.VMEM((n_all, chunk, rank), BF16),
            pltpu.VMEM((feats, cols), F32),
            pltpu.VMEM((feats, cols), BF16),
            pltpu.VMEM((feats, cols), BF16),
            pltpu.VMEM((docs, slots), BF16),
            pltpu.VMEM((slots, rank), F32),
            pltpu.VMEM((slots, rank), F32),
            pltpu.VMEM((slots, rank), F32),
            pltpu.VMEM((slots, rank), F32),
            pltpu.VMEM((n_col, docs, rank), F32),
            pltpu.VMEM((n_col, docs, rank), BF16),
            pltpu.VMEM((n_col, docs, rank), BF16),
            pltpu.VMEM((ny, NZ, rows, cols), F32),
            pltpu.VMEM((CHUNKS, NZ - 1, NZ, rows, cols // CHUNKS), F32),
            pltpu.VMEM((CHUNKS, NZ, rows, cols // CHUNKS), F32),
            pltpu.VMEM((CHUNKS, NZ - 1, rows, cols // CHUNKS), F32),
            dma((n_all,)), dma((n_all,)), dma,
            dma((n_row,)), dma((n_row,)), dma((n_col,)), dma((n_col,)),
            dma((nx,)), dma((nx,)), dma((nx,)), dma((nx,)),
            dma((CHUNKS, NZ)), dma((CHUNKS, NZ)), dma((CHUNKS, NZ)), dma((CHUNKS, NZ)),
        ],
        compiler_params=pltpu.CompilerParams(
            collective_id=0, has_side_effects=True, vmem_limit_bytes=56 << 20
        ),
    )(
        saved_inputs, output_grads, proj_in, proj_out,
        doc_lengths.reshape(1, docs), device_docs.reshape(1, docs), fisher_inverse,
    )


def solution(mesh):
    placed = (P(("row", "col"), None), P(("row", "col"), None), P(), P(), P(), P(), P("row", "col"))
    return jax.shard_map(
        per_device, mesh=mesh, in_specs=placed, out_specs=P("row", "col"), check_vma=False
    )
```

```python
import jax
import jax.numpy as jnp
from jax import lax
from jax.experimental import pallas as pl
from jax.experimental.pallas import tpu as pltpu
from jax.sharding import PartitionSpec as P

SLOTS = 5
PAD = 8
CORES = 2
NZ = 4
CHUNKS = 4
F32 = jnp.float32
BF16 = jnp.bfloat16
MESH = pl.DeviceIdType.MESH


def split(x):
    hi = x.astype(BF16)
    return hi, (x - hi.astype(F32)).astype(BF16)


def dot(a, b):
    return jnp.dot(a, b, preferred_element_type=F32)


def body(
    chunk, si, og, pi, po, dl, dd, fi, out,
    x, w, f32buf, fhi, flo, sel, pbuf, tbuf, gbuf, ghi, glo, ybuf, mbuf, qbuf, obuf,
    x_sem, w_sem, f_sem, s1, r1, s3, r3, s5, r5, s4, r4, s6, r6,
):
    n_row = lax.axis_size("row")
    n_col = lax.axis_size("col")
    row = lax.axis_index("row")
    col = lax.axis_index("col")
    tok, d_in = si.shape
    rank = pi.shape[1]
    docs = dl.shape[1]
    n_in = d_in // chunk
    n_all = n_in + og.shape[1] // chunk
    n_dev = n_row * n_col
    me = row * n_col + col

    def each_other(act):
        for lo, hi in ((n_row // 2, n_row), (1, n_row // 2)):
            @pl.loop(lo, hi)
            def _(j):
                to = lax.rem(row + j, n_row)
                for c in range(n_col):
                    act(to, c)

        @pl.loop(1, n_col)
        def _(j):
            act(row, lax.rem(col + j, n_col))

    loads = []
    for k in range(n_all):
        a, b, i = (si, pi, k) if k < n_in else (og, po, k - n_in)
        cols = pl.ds(i * chunk, chunk)
        loads.append((
            pltpu.make_async_copy(a.at[:, cols], x.at[k], x_sem.at[k]),
            pltpu.make_async_copy(b.at[cols, :], w.at[k], w_sem.at[k]),
        ))
        for c in loads[-1]:
            c.start()
    f_load = pltpu.make_async_copy(fi, f32buf, f_sem)
    f_load.start()

    barrier = pltpu.get_barrier_semaphore()

    def greet(to_row, to_col):
        pl.semaphore_signal(barrier, inc=1, device_id={"row": to_row, "col": to_col}, device_id_type=MESH)

    each_other(greet)

    lens = jnp.broadcast_to(dl[...].astype(F32), (docs, docs))
    down = lax.broadcasted_iota(jnp.int32, (docs, docs), 0)
    along = lax.broadcasted_iota(jnp.int32, (docs, docs), 1)
    starts_col = jnp.sum(jnp.where(along < down, lens, 0.0), axis=1, keepdims=True)
    starts_row = jnp.sum(jnp.where(down == along, starts_col, 0.0), axis=0, keepdims=True)
    owner_col = jnp.sum(jnp.where(down == along, dd[...].astype(F32), 0.0), axis=1, keepdims=True)

    lanes = lax.broadcasted_iota(jnp.int32, (1, SLOTS * n_dev), 1)
    first = jnp.sum(jnp.where(starts_col <= (lax.rem(lanes, n_dev) * tok).astype(F32), 1.0, 0.0), axis=0, keepdims=True) - 1.0
    slot_doc = first + (lanes // n_dev).astype(F32)
    sel[...] = jnp.where(owner_col == slot_doc, 1.0, 0.0).astype(BF16)

    base = me * tok
    pos = base + lax.broadcasted_iota(jnp.int32, (tok, 1), 0)
    begun = (starts_row <= pos.astype(F32)) & (starts_row > jnp.full((1, 1), base, jnp.int32).astype(F32))
    slot = jnp.sum(jnp.where(begun, 1.0, 0.0), axis=1, keepdims=True)

    low = []
    for lo, hi in ((0, n_in), (n_in, n_all)):
        acc = None
        for k in range(lo, hi):
            for c in loads[k]:
                c.wait()
            term = dot(x[k], w[k])
            acc = term if acc is None else acc + term
        low.append(acc.astype(BF16))
    low_in, low_out = low
    masked = jnp.concatenate(
        [jnp.where(slot == float(s), low_in, jnp.zeros_like(low_in)) for s in range(SLOTS)], axis=1
    )
    part = lax.dot_general(low_out, masked, (((0,), (0,)), ((), ())), preferred_element_type=F32)
    for s in range(SLOTS):
        pbuf[pl.ds(s, rank, stride=PAD), :] = part[:, s * rank:(s + 1) * rank]

    pl.semaphore_wait(barrier, n_dev - 1)

    def slots_of(ref, i):
        return ref.at[pl.ds(pl.multiple_of(i * PAD, PAD), SLOTS), :]

    def give(to_row, to_col):
        pltpu.make_async_remote_copy(
            src_ref=slots_of(pbuf, to_row * n_col + to_col), dst_ref=slots_of(tbuf, me), send_sem=s1, recv_sem=r1,
            device_id={"row": to_row, "col": to_col}, device_id_type=MESH,
        ).start()

    each_other(give)

    at = pl.ds(pl.multiple_of(me * PAD, PAD), SLOTS)
    tbuf[at, :] = pbuf[at, :]

    f_load.wait()

    @pl.loop(0, fi.shape[0] // 32)
    def _(i):
        at = pl.ds(pl.multiple_of(i * 32, 32), 32)
        fhi[at, :], flo[at, :] = split(f32buf[at, :])

    others = pl.ds(0, (n_dev - 1) * SLOTS)
    pltpu.make_async_copy(tbuf.at[others, :], tbuf.at[others, :], r1).wait()

    t_hi, t_lo = split(jnp.concatenate([tbuf[pl.ds(s, n_dev, stride=PAD), :] for s in range(SLOTS)], axis=0))
    gbuf[col] = dot(sel[...], t_hi) + dot(sel[...], t_lo)

    nx = n_col // CORES
    cx = col // CORES
    core = lax.rem(col, CORES)
    sibling = col + 1 - 2 * core

    def hand(at, to, send, recv):
        return pltpu.make_async_remote_copy(
            src_ref=gbuf.at[at], dst_ref=gbuf.at[at], send_sem=send, recv_sem=recv,
            device_id={"row": row, "col": to}, device_id_type=MESH,
        )

    def keep(at):
        ghi[at], glo[at] = split(gbuf[at])

    around = [hand(col, lax.rem(cx + j, nx) * CORES + core, s3.at[j], r3.at[j]) for j in range(1, nx)]
    across = [hand(col, sibling, s5.at[0], r5.at[0])]
    for c in around + across:
        c.start()
    keep(col)
    for j in range(1, nx):
        around[j - 1].wait_recv()
        at = lax.rem(cx + nx - j, nx) * CORES + core
        across.append(hand(at, sibling, s5.at[j], r5.at[j]))
        across[j].start()
        keep(at)
    for j in range(nx):
        across[j].wait_recv()
        keep(lax.rem(cx + nx - j, nx) * CORES + 1 - core)

    ny = n_row // NZ
    y, z = row // NZ, lax.rem(row, NZ)
    rows = docs // n_row
    wide = ybuf.shape[3] // CHUNKS
    g_hi = jnp.concatenate([ghi[c] for c in range(n_col)], axis=1)
    g_lo = jnp.concatenate([glo[c] for c in range(n_col)], axis=1)

    def peer(along_y, j):
        if along_y:
            to = lax.rem(y + j, ny)
            return to, {"row": to * NZ + z, "col": col}
        to = lax.rem(z + j, NZ)
        return to, {"row": y * NZ + to, "col": col}

    first_hop, second_hop = [], []
    for n in range(CHUNKS):
        cols = slice(n * wide, (n + 1) * wide)
        f_hi, f_lo = fhi[:, cols], flo[:, cols]
        prod = dot(g_hi, f_hi) + (dot(g_hi, f_lo) + dot(g_lo, f_hi))
        ybuf[:, :, :, cols] = prod.reshape(ny, NZ, rows, wide)
        hops = []
        for j in range(1, ny if n % 2 == 0 else NZ):
            to, device = peer(n % 2 == 0, j)
            src = ybuf.at[to, :, :, cols] if n % 2 == 0 else ybuf.at[:, to, :, cols]
            hops.append(pltpu.make_async_remote_copy(
                src_ref=src, dst_ref=mbuf.at[n, j - 1], send_sem=s4.at[n, j], recv_sem=r4.at[n, j],
                device_id=device, device_id_type=MESH,
            ))
            hops[-1].start()
        first_hop.append(hops)

    for n in range(CHUNKS):
        cols = slice(n * wide, (n + 1) * wide)
        part = ybuf[y, :, :, cols] if n % 2 == 0 else ybuf[:, z, :, cols]
        for j, c in enumerate(first_hop[n]):
            c.wait_recv()
            part = part + mbuf[n, j]
        qbuf[n] = part
        hops = []
        for j in range(1, NZ if n % 2 == 0 else ny):
            to, device = peer(n % 2 == 1, j)
            hops.append(pltpu.make_async_remote_copy(
                src_ref=qbuf.at[n, to], dst_ref=obuf.at[n, j - 1], send_sem=s6.at[n, j], recv_sem=r6.at[n, j],
                device_id=device, device_id_type=MESH,
            ))
            hops[-1].start()
        second_hop.append(hops)

    for n in range(CHUNKS):
        total = qbuf[n, z if n % 2 == 0 else y]
        for j, c in enumerate(second_hop[n]):
            c.wait_recv()
            total = total + obuf[n, j]
        out[:, n * wide:(n + 1) * wide] = total

    pltpu.make_async_copy(pbuf.at[others, :], pbuf.at[others, :], s1).wait()
    for c in around + across + sum(first_hop + second_hop, []):
        c.wait_send()


def per_device(saved_inputs, output_grads, proj_in, proj_out, doc_lengths, device_docs, fisher_inverse):
    n_row, n_col = lax.axis_size("row"), lax.axis_size("col")
    tok, d_in = saved_inputs.shape
    ff = output_grads.shape[1]
    rank = proj_in.shape[1]
    docs = doc_lengths.shape[0]
    feats, cols = fisher_inverse.shape
    chunk = 2048
    n_all = (d_in + ff) // chunk
    slots = n_row * n_col * SLOTS
    ny, nx, rows = n_row // NZ, n_col // CORES, docs // n_row
    dma = pltpu.SemaphoreType.DMA
    hbm = pl.BlockSpec(memory_space=pl.ANY)
    vmem = pl.BlockSpec(memory_space=pltpu.VMEM)

    def kernel(*refs):
        body(chunk, *refs)

    return pl.pallas_call(
        kernel,
        out_shape=jax.ShapeDtypeStruct((docs // n_row, cols), F32),
        in_specs=[hbm, hbm, hbm, hbm, vmem, vmem, hbm],
        out_specs=vmem,
        scratch_shapes=[
            pltpu.VMEM((n_all, tok, chunk), BF16),
            pltpu.VMEM((n_all, chunk, rank), BF16),
            pltpu.VMEM((feats, cols), F32),
            pltpu.VMEM((feats, cols), BF16),
            pltpu.VMEM((feats, cols), BF16),
            pltpu.VMEM((docs, slots), BF16),
            pltpu.VMEM((n_row * n_col * PAD, rank), F32),
            pltpu.VMEM((n_row * n_col * PAD, rank), F32),
            pltpu.VMEM((n_col, docs, rank), F32),
            pltpu.VMEM((n_col, docs, rank), BF16),
            pltpu.VMEM((n_col, docs, rank), BF16),
            pltpu.VMEM((ny, NZ, rows, cols), F32),
            pltpu.VMEM((CHUNKS, NZ - 1, NZ, rows, cols // CHUNKS), F32),
            pltpu.VMEM((CHUNKS, NZ, rows, cols // CHUNKS), F32),
            pltpu.VMEM((CHUNKS, NZ - 1, rows, cols // CHUNKS), F32),
            dma((n_all,)), dma((n_all,)), dma,
            dma, dma,
            dma((nx,)), dma((nx,)), dma((nx,)), dma((nx,)),
            dma((CHUNKS, NZ)), dma((CHUNKS, NZ)), dma((CHUNKS, NZ)), dma((CHUNKS, NZ)),
        ],
        compiler_params=pltpu.CompilerParams(
            collective_id=0, has_side_effects=True, vmem_limit_bytes=56 << 20
        ),
    )(
        saved_inputs, output_grads, proj_in, proj_out,
        doc_lengths.reshape(1, docs), device_docs.reshape(1, docs), fisher_inverse,
    )


def solution(mesh):
    placed = (P(("row", "col"), None), P(("row", "col"), None), P(), P(), P(), P(), P("row", "col"))
    return jax.shard_map(
        per_device, mesh=mesh, in_specs=placed, out_specs=P("row", "col"), check_vma=False
    )
```

```python
import jax
import jax.numpy as jnp
from jax import lax
from jax.experimental import pallas as pl
from jax.experimental.pallas import tpu as pltpu
from jax.sharding import PartitionSpec as P

SLOTS = 5
PAD = 8
CORES = 2
NZ = 4
CHUNKS = 4
F32 = jnp.float32
BF16 = jnp.bfloat16
MESH = pl.DeviceIdType.MESH


def split(x):
    hi = x.astype(BF16)
    return hi, (x - hi.astype(F32)).astype(BF16)


def dot(a, b):
    return jnp.dot(a, b, preferred_element_type=F32)


def body(
    chunk, si, og, pi, po, dl, dd, fi, out,
    x, w, f32buf, fhi, flo, sel, pbuf, tbuf, gbuf, ghi, glo, ybuf, mbuf, qbuf, obuf,
    x_sem, w_sem, f_sem, s1, r1, s3, r3, s5, r5, s4, r4, s6, r6,
):
    n_row = lax.axis_size("row")
    n_col = lax.axis_size("col")
    row = lax.axis_index("row")
    col = lax.axis_index("col")
    tok, d_in = si.shape
    rank = pi.shape[1]
    docs = dl.shape[1]
    n_in = d_in // chunk
    n_all = n_in + og.shape[1] // chunk
    n_dev = n_row * n_col
    me = row * n_col + col

    def each_other(act):
        for lo, hi in ((n_row // 2, n_row), (1, n_row // 2)):
            @pl.loop(lo, hi)
            def _(j):
                to = lax.rem(row + j, n_row)
                for c in range(n_col):
                    act(to, c)

        @pl.loop(1, n_col)
        def _(j):
            act(row, lax.rem(col + j, n_col))

    loads = []
    for k in range(n_all):
        a, b, i = (si, pi, k) if k < n_in else (og, po, k - n_in)
        cols = pl.ds(i * chunk, chunk)
        loads.append((
            pltpu.make_async_copy(a.at[:, cols], x.at[k], x_sem.at[k]),
            pltpu.make_async_copy(b.at[cols, :], w.at[k], w_sem.at[k]),
        ))
        for c in loads[-1]:
            c.start()
    f_load = pltpu.make_async_copy(fi, f32buf, f_sem)
    f_load.start()

    barrier = pltpu.get_barrier_semaphore()

    def greet(to_row, to_col):
        pl.semaphore_signal(barrier, inc=1, device_id={"row": to_row, "col": to_col}, device_id_type=MESH)

    each_other(greet)

    lens = jnp.broadcast_to(dl[...].astype(F32), (docs, docs))
    down = lax.broadcasted_iota(jnp.int32, (docs, docs), 0)
    along = lax.broadcasted_iota(jnp.int32, (docs, docs), 1)
    starts_col = jnp.sum(jnp.where(along < down, lens, 0.0), axis=1, keepdims=True)
    starts_row = jnp.sum(jnp.where(down == along, starts_col, 0.0), axis=0, keepdims=True)
    owner_col = jnp.sum(jnp.where(down == along, dd[...].astype(F32), 0.0), axis=1, keepdims=True)

    lanes = lax.broadcasted_iota(jnp.int32, (1, SLOTS * n_dev), 1)
    first = jnp.sum(jnp.where(starts_col <= (lax.rem(lanes, n_dev) * tok).astype(F32), 1.0, 0.0), axis=0, keepdims=True) - 1.0
    slot_doc = first + (lanes // n_dev).astype(F32)
    sel[...] = jnp.where(owner_col == slot_doc, 1.0, 0.0).astype(BF16)

    base = me * tok
    pos = base + lax.broadcasted_iota(jnp.int32, (tok, 1), 0)
    begun = (starts_row <= pos.astype(F32)) & (starts_row > jnp.full((1, 1), base, jnp.int32).astype(F32))
    slot = jnp.sum(jnp.where(begun, 1.0, 0.0), axis=1, keepdims=True)

    low = []
    for lo, hi in ((0, n_in), (n_in, n_all)):
        acc = None
        for k in range(lo, hi):
            for c in loads[k]:
                c.wait()
            term = dot(x[k], w[k])
            acc = term if acc is None else acc + term
        low.append(acc.astype(BF16))
    low_in, low_out = low
    masked = jnp.concatenate(
        [jnp.where(slot == float(s), low_in, jnp.zeros_like(low_in)) for s in range(SLOTS)], axis=1
    )
    part = lax.dot_general(low_out, masked, (((0,), (0,)), ((), ())), preferred_element_type=F32)
    for s in range(SLOTS):
        pbuf[pl.ds(s, rank, stride=PAD), :] = part[:, s * rank:(s + 1) * rank]

    pl.semaphore_wait(barrier, n_dev - 1)

    def slots_of(ref, i):
        return ref.at[pl.ds(pl.multiple_of(i * PAD, PAD), SLOTS), :]

    def give(to_row, to_col):
        pltpu.make_async_remote_copy(
            src_ref=slots_of(pbuf, to_row * n_col + to_col), dst_ref=slots_of(tbuf, me), send_sem=s1, recv_sem=r1,
            device_id={"row": to_row, "col": to_col}, device_id_type=MESH,
        ).start()

    each_other(give)

    at = pl.ds(pl.multiple_of(me * PAD, PAD), SLOTS)
    tbuf[at, :] = pbuf[at, :]

    f_load.wait()

    @pl.loop(0, fi.shape[0] // 32)
    def _(i):
        at = pl.ds(pl.multiple_of(i * 32, 32), 32)
        fhi[at, :], flo[at, :] = split(f32buf[at, :])

    others = pl.ds(0, (n_dev - 1) * SLOTS)
    pltpu.make_async_copy(tbuf.at[others, :], tbuf.at[others, :], r1).wait()

    t_hi, t_lo = split(jnp.concatenate([tbuf[pl.ds(s, n_dev, stride=PAD), :] for s in range(SLOTS)], axis=0))
    gbuf[col] = dot(sel[...], t_hi) + dot(sel[...], t_lo)

    nx = n_col // CORES
    cx = col // CORES
    core = lax.rem(col, CORES)
    sibling = col + 1 - 2 * core

    def hand(at, to, send, recv):
        return pltpu.make_async_remote_copy(
            src_ref=gbuf.at[at], dst_ref=gbuf.at[at], send_sem=send, recv_sem=recv,
            device_id={"row": row, "col": to}, device_id_type=MESH,
        )

    def keep(at):
        ghi[at], glo[at] = split(gbuf[at])

    around = [hand(col, lax.rem(cx + j, nx) * CORES + core, s3.at[j], r3.at[j]) for j in range(1, nx)]
    across = [hand(col, sibling, s5.at[0], r5.at[0])]
    for c in around + across:
        c.start()
    keep(col)
    for j in range(1, nx):
        around[j - 1].wait_recv()
        at = lax.rem(cx + nx - j, nx) * CORES + core
        across.append(hand(at, sibling, s5.at[j], r5.at[j]))
        across[j].start()
        keep(at)
    for j in range(nx):
        across[j].wait_recv()
        keep(lax.rem(cx + nx - j, nx) * CORES + 1 - core)

    ny = n_row // NZ
    y, z = row // NZ, lax.rem(row, NZ)
    rows = docs // n_row
    wide = ybuf.shape[3] // CHUNKS
    g_hi = jnp.concatenate([ghi[c] for c in range(n_col)], axis=1)
    g_lo = jnp.concatenate([glo[c] for c in range(n_col)], axis=1)

    def peer(along_y, j):
        if along_y:
            to = lax.rem(y + j, ny)
            return to, {"row": to * NZ + z, "col": col}
        to = lax.rem(z + j, NZ)
        return to, {"row": y * NZ + to, "col": col}

    first_hop, second_hop = [], []
    for n in range(CHUNKS):
        cols = slice(n * wide, (n + 1) * wide)
        f_hi, f_lo = fhi[:, cols], flo[:, cols]
        prod = dot(g_hi, f_hi) + (dot(g_hi, f_lo) + dot(g_lo, f_hi))
        ybuf[:, :, :, cols] = prod.reshape(ny, NZ, rows, wide)
        hops = []
        for j in range(1, ny if n % 2 == 0 else NZ):
            to, device = peer(n % 2 == 0, j)
            src = ybuf.at[to, :, :, cols] if n % 2 == 0 else ybuf.at[:, to, :, cols]
            hops.append(pltpu.make_async_remote_copy(
                src_ref=src, dst_ref=mbuf.at[n, j - 1], send_sem=s4.at[n, j], recv_sem=r4.at[n, j],
                device_id=device, device_id_type=MESH,
            ))
            hops[-1].start()
        first_hop.append(hops)

    for n in range(CHUNKS):
        cols = slice(n * wide, (n + 1) * wide)
        part = ybuf[y, :, :, cols] if n % 2 == 0 else ybuf[:, z, :, cols]
        for j, c in enumerate(first_hop[n]):
            c.wait_recv()
            part = part + mbuf[n, j]
        qbuf[n] = part
        hops = []
        for j in range(1, NZ if n % 2 == 0 else ny):
            to, device = peer(n % 2 == 1, j)
            hops.append(pltpu.make_async_remote_copy(
                src_ref=qbuf.at[n, to], dst_ref=obuf.at[n, j - 1], send_sem=s6.at[n, j], recv_sem=r6.at[n, j],
                device_id=device, device_id_type=MESH,
            ))
            hops[-1].start()
        second_hop.append(hops)

    for n in range(CHUNKS):
        total = qbuf[n, z if n % 2 == 0 else y]
        for j, c in enumerate(second_hop[n]):
            c.wait_recv()
            total = total + obuf[n, j]
        out[:, n * wide:(n + 1) * wide] = total

    pltpu.make_async_copy(pbuf.at[others, :], pbuf.at[others, :], s1).wait()
    for c in around + across + sum(first_hop + second_hop, []):
        c.wait_send()


def per_device(saved_inputs, output_grads, proj_in, proj_out, doc_lengths, device_docs, fisher_inverse):
    n_row, n_col = lax.axis_size("row"), lax.axis_size("col")
    tok, d_in = saved_inputs.shape
    ff = output_grads.shape[1]
    rank = proj_in.shape[1]
    docs = doc_lengths.shape[0]
    feats, cols = fisher_inverse.shape
    chunk = 2048
    n_all = (d_in + ff) // chunk
    slots = n_row * n_col * SLOTS
    ny, nx, rows = n_row // NZ, n_col // CORES, docs // n_row
    dma = pltpu.SemaphoreType.DMA
    hbm = pl.BlockSpec(memory_space=pl.ANY)
    vmem = pl.BlockSpec(memory_space=pltpu.VMEM)

    def kernel(*refs):
        body(chunk, *refs)

    return pl.pallas_call(
        kernel,
        out_shape=pltpu.VMEM((docs // n_row, cols), F32),
        in_specs=[hbm, hbm, hbm, hbm, vmem, vmem, hbm],
        out_specs=vmem,
        scratch_shapes=[
            pltpu.VMEM((n_all, tok, chunk), BF16),
            pltpu.VMEM((n_all, chunk, rank), BF16),
            pltpu.VMEM((feats, cols), F32),
            pltpu.VMEM((feats, cols), BF16),
            pltpu.VMEM((feats, cols), BF16),
            pltpu.VMEM((docs, slots), BF16),
            pltpu.VMEM((n_row * n_col * PAD, rank), F32),
            pltpu.VMEM((n_row * n_col * PAD, rank), F32),
            pltpu.VMEM((n_col, docs, rank), F32),
            pltpu.VMEM((n_col, docs, rank), BF16),
            pltpu.VMEM((n_col, docs, rank), BF16),
            pltpu.VMEM((ny, NZ, rows, cols), F32),
            pltpu.VMEM((CHUNKS, NZ - 1, NZ, rows, cols // CHUNKS), F32),
            pltpu.VMEM((CHUNKS, NZ, rows, cols // CHUNKS), F32),
            pltpu.VMEM((CHUNKS, NZ - 1, rows, cols // CHUNKS), F32),
            dma((n_all,)), dma((n_all,)), dma,
            dma, dma,
            dma((nx,)), dma((nx,)), dma((nx,)), dma((nx,)),
            dma((CHUNKS, NZ)), dma((CHUNKS, NZ)), dma((CHUNKS, NZ)), dma((CHUNKS, NZ)),
        ],
        compiler_params=pltpu.CompilerParams(
            collective_id=0, has_side_effects=True, vmem_limit_bytes=56 << 20
        ),
    )(
        saved_inputs, output_grads, proj_in, proj_out,
        doc_lengths.reshape(1, docs), device_docs.reshape(1, docs), fisher_inverse,
    )


def solution(mesh):
    placed = (P(("row", "col"), None), P(("row", "col"), None), P(), P(), P(), P(), P("row", "col"))
    return jax.shard_map(
        per_device, mesh=mesh, in_specs=placed, out_specs=P("row", "col"), check_vma=False
    )
```

```python
import jax
import jax.numpy as jnp
from jax import lax
from jax.experimental import pallas as pl
from jax.experimental.pallas import tpu as pltpu
from jax.sharding import PartitionSpec as P

SLOTS = 5
PAD = 8
CORES = 2
NZ = 4
WIDTHS = (1, 1, 2, 2, 1, 1)
CHUNKS = len(WIDTHS)
EARLY = 2
F32 = jnp.float32
BF16 = jnp.bfloat16
MESH = pl.DeviceIdType.MESH


def split(x):
    hi = x.astype(BF16)
    return hi, (x - hi.astype(F32)).astype(BF16)


def dot(a, b):
    return jnp.dot(a, b, preferred_element_type=F32)


def body(
    chunk, si, og, pi, po, dl, dd, fi, out,
    x, w, f32buf, fhi, flo, sel, pbuf, tbuf, gbuf, ghi, glo, ybuf, mbuf, qbuf, obuf,
    x_sem, w_sem, f_sem, s1, r1, s3, r3, s5, r5, s4, r4, s6, r6,
):
    n_row = lax.axis_size("row")
    n_col = lax.axis_size("col")
    row = lax.axis_index("row")
    col = lax.axis_index("col")
    tok, d_in = si.shape
    rank = pi.shape[1]
    docs = dl.shape[1]
    n_in = d_in // chunk
    n_all = n_in + og.shape[1] // chunk
    n_dev = n_row * n_col
    me = row * n_col + col

    def each_other(act):
        for lo, hi in ((n_row // 2, n_row), (1, n_row // 2)):
            @pl.loop(lo, hi)
            def _(j):
                to = lax.rem(row + j, n_row)
                for c in range(n_col):
                    act(to, c)

        @pl.loop(1, n_col)
        def _(j):
            act(row, lax.rem(col + j, n_col))

    loads = []
    for k in range(n_all):
        a, b, i = (si, pi, k) if k < n_in else (og, po, k - n_in)
        cols = pl.ds(i * chunk, chunk)
        loads.append((
            pltpu.make_async_copy(a.at[:, cols], x.at[k], x_sem.at[k]),
            pltpu.make_async_copy(b.at[cols, :], w.at[k], w_sem.at[k]),
        ))
        for c in loads[-1]:
            c.start()
    f_load = pltpu.make_async_copy(fi, f32buf, f_sem)
    f_load.start()

    barrier = pltpu.get_barrier_semaphore()

    def greet(to_row, to_col):
        pl.semaphore_signal(barrier, inc=1, device_id={"row": to_row, "col": to_col}, device_id_type=MESH)

    each_other(greet)

    lens = jnp.broadcast_to(dl[...].astype(F32), (docs, docs))
    down = lax.broadcasted_iota(jnp.int32, (docs, docs), 0)
    along = lax.broadcasted_iota(jnp.int32, (docs, docs), 1)
    starts_col = jnp.sum(jnp.where(along < down, lens, 0.0), axis=1, keepdims=True)
    starts_row = jnp.sum(jnp.where(down == along, starts_col, 0.0), axis=0, keepdims=True)

    base = me * tok
    pos = base + lax.broadcasted_iota(jnp.int32, (tok, 1), 0)
    begun = (starts_row <= pos.astype(F32)) & (starts_row > jnp.full((1, 1), base, jnp.int32).astype(F32))
    slot = jnp.sum(jnp.where(begun, 1.0, 0.0), axis=1, keepdims=True)

    low = []
    for lo, hi in ((0, n_in), (n_in, n_all)):
        acc = None
        for k in range(lo, hi):
            for c in loads[k]:
                c.wait()
            term = dot(x[k], w[k])
            acc = term if acc is None else acc + term
        low.append(acc.astype(BF16))
    low_in, low_out = low
    masked = jnp.concatenate(
        [jnp.where(slot == float(s), low_in, jnp.zeros_like(low_in)) for s in range(SLOTS)], axis=1
    )
    part = lax.dot_general(low_out, masked, (((0,), (0,)), ((), ())), preferred_element_type=F32)
    for s in range(SLOTS):
        pbuf[pl.ds(s, rank, stride=PAD), :] = part[:, s * rank:(s + 1) * rank]

    pl.semaphore_wait(barrier, n_dev - 1)

    def slots_of(ref, i):
        return ref.at[pl.ds(pl.multiple_of(i * PAD, PAD), SLOTS), :]

    def give(to_row, to_col):
        pltpu.make_async_remote_copy(
            src_ref=slots_of(pbuf, to_row * n_col + to_col), dst_ref=slots_of(tbuf, me), send_sem=s1, recv_sem=r1,
            device_id={"row": to_row, "col": to_col}, device_id_type=MESH,
        ).start()

    each_other(give)

    at = pl.ds(pl.multiple_of(me * PAD, PAD), SLOTS)
    tbuf[at, :] = pbuf[at, :]

    owner_col = jnp.sum(jnp.where(down == along, dd[...].astype(F32), 0.0), axis=1, keepdims=True)

    lanes = lax.broadcasted_iota(jnp.int32, (1, SLOTS * n_dev), 1)
    first = jnp.sum(jnp.where(starts_col <= (lax.rem(lanes, n_dev) * tok).astype(F32), 1.0, 0.0), axis=0, keepdims=True) - 1.0
    slot_doc = first + (lanes // n_dev).astype(F32)
    sel[...] = jnp.where(owner_col == slot_doc, 1.0, 0.0).astype(BF16)

    f_load.wait()

    @pl.loop(0, fi.shape[0] // 32)
    def _(i):
        at = pl.ds(pl.multiple_of(i * 32, 32), 32)
        fhi[at, :], flo[at, :] = split(f32buf[at, :])

    others = pl.ds(0, (n_dev - 1) * SLOTS)
    pltpu.make_async_copy(tbuf.at[others, :], tbuf.at[others, :], r1).wait()

    t_hi, t_lo = split(jnp.concatenate([tbuf[pl.ds(s, n_dev, stride=PAD), :] for s in range(SLOTS)], axis=0))
    gbuf[col] = dot(sel[...], t_hi) + dot(sel[...], t_lo)

    nx = n_col // CORES
    cx = col // CORES
    core = lax.rem(col, CORES)
    sibling = col + 1 - 2 * core

    def hand(at, to, send, recv):
        return pltpu.make_async_remote_copy(
            src_ref=gbuf.at[at], dst_ref=gbuf.at[at], send_sem=send, recv_sem=recv,
            device_id={"row": row, "col": to}, device_id_type=MESH,
        )

    def keep(at):
        ghi[at], glo[at] = split(gbuf[at])

    around = [hand(col, lax.rem(cx + j, nx) * CORES + core, s3.at[j], r3.at[j]) for j in range(1, nx)]
    across = [hand(col, sibling, s5.at[0], r5.at[0])]
    for c in around + across:
        c.start()
    keep(col)
    for j in range(1, nx):
        around[j - 1].wait_recv()
        at = lax.rem(cx + nx - j, nx) * CORES + core
        across.append(hand(at, sibling, s5.at[j], r5.at[j]))
        across[j].start()
        keep(at)
    def product(side, cols):
        at = [x * CORES + side for x in range(nx)]
        a_hi, a_lo = (jnp.concatenate([b[c] for c in at], axis=1) for b in (ghi, glo))
        b_hi, b_lo = (
            jnp.concatenate([b[pl.ds(pl.multiple_of(c * rank, rank), rank), cols] for c in at], axis=0) for b in (fhi, flo)
        )
        return dot(a_hi, b_hi) + (dot(a_hi, b_lo) + dot(a_lo, b_hi))

    unit = ybuf.shape[3] // sum(WIDTHS)
    begin = [unit * sum(WIDTHS[:n]) for n in range(CHUNKS + 1)]
    for n in range(EARLY):
        cols = slice(begin[n], begin[n + 1])
        ybuf[:, :, :, cols] = product(core, cols).reshape(n_row // NZ, NZ, docs // n_row, begin[n + 1] - begin[n])
    for j in range(nx):
        across[j].wait_recv()
        keep(lax.rem(cx + nx - j, nx) * CORES + 1 - core)

    ny = n_row // NZ
    y, z = row // NZ, lax.rem(row, NZ)
    rows = docs // n_row
    g_hi = jnp.concatenate([ghi[c] for c in range(n_col)], axis=1)
    g_lo = jnp.concatenate([glo[c] for c in range(n_col)], axis=1)

    def peer(along_y, j):
        if along_y:
            to = lax.rem(y + j, ny)
            return to, {"row": to * NZ + z, "col": col}
        to = lax.rem(z + j, NZ)
        return to, {"row": y * NZ + to, "col": col}

    first_hop, second_hop = [], []
    for n in range(CHUNKS):
        cols = slice(begin[n], begin[n + 1])
        wide = begin[n + 1] - begin[n]
        if n < EARLY:
            ybuf[:, :, :, cols] += product(1 - core, cols).reshape(ny, NZ, rows, wide)
        else:
            f_hi, f_lo = fhi[:, cols], flo[:, cols]
            prod = dot(g_hi, f_hi) + (dot(g_hi, f_lo) + dot(g_lo, f_hi))
            ybuf[:, :, :, cols] = prod.reshape(ny, NZ, rows, wide)
        hops = []
        for j in range(1, ny if n % 2 == 0 else NZ):
            to, device = peer(n % 2 == 0, j)
            src = ybuf.at[to, :, :, cols] if n % 2 == 0 else ybuf.at[:, to, :, cols]
            hops.append(pltpu.make_async_remote_copy(
                src_ref=src, dst_ref=mbuf.at[n, j - 1, :, :, 0:wide], send_sem=s4.at[n, j], recv_sem=r4.at[n, j],
                device_id=device, device_id_type=MESH,
            ))
            hops[-1].start()
        first_hop.append(hops)

    for n in range(CHUNKS):
        cols = slice(begin[n], begin[n + 1])
        wide = begin[n + 1] - begin[n]
        part = ybuf[y, :, :, cols] if n % 2 == 0 else ybuf[:, z, :, cols]
        for j, c in enumerate(first_hop[n]):
            c.wait_recv()
            part = part + mbuf[n, j, :, :, 0:wide]
        qbuf[n, :, :, 0:wide] = part
        hops = []
        for j in range(1, NZ if n % 2 == 0 else ny):
            to, device = peer(n % 2 == 1, j)
            hops.append(pltpu.make_async_remote_copy(
                src_ref=qbuf.at[n, to, :, 0:wide], dst_ref=obuf.at[n, j - 1, :, 0:wide], send_sem=s6.at[n, j], recv_sem=r6.at[n, j],
                device_id=device, device_id_type=MESH,
            ))
            hops[-1].start()
        second_hop.append(hops)

    for n in range(CHUNKS):
        wide = begin[n + 1] - begin[n]
        total = qbuf[n, z if n % 2 == 0 else y, :, 0:wide]
        for j, c in enumerate(second_hop[n]):
            c.wait_recv()
            total = total + obuf[n, j, :, 0:wide]
        out[:, begin[n]:begin[n + 1]] = total

    pltpu.make_async_copy(pbuf.at[others, :], pbuf.at[others, :], s1).wait()
    for c in around + across + sum(first_hop + second_hop, []):
        c.wait_send()


def per_device(saved_inputs, output_grads, proj_in, proj_out, doc_lengths, device_docs, fisher_inverse):
    n_row, n_col = lax.axis_size("row"), lax.axis_size("col")
    tok, d_in = saved_inputs.shape
    ff = output_grads.shape[1]
    rank = proj_in.shape[1]
    docs = doc_lengths.shape[0]
    feats, cols = fisher_inverse.shape
    chunk = 2048
    n_all = (d_in + ff) // chunk
    slots = n_row * n_col * SLOTS
    ny, nx, rows = n_row // NZ, n_col // CORES, docs // n_row
    dma = pltpu.SemaphoreType.DMA
    hbm = pl.BlockSpec(memory_space=pl.ANY)
    vmem = pl.BlockSpec(memory_space=pltpu.VMEM)

    def kernel(*refs):
        body(chunk, *refs)

    return pl.pallas_call(
        kernel,
        out_shape=pltpu.VMEM((docs // n_row, cols), F32),
        in_specs=[hbm, hbm, hbm, hbm, vmem, vmem, hbm],
        out_specs=vmem,
        scratch_shapes=[
            pltpu.VMEM((n_all, tok, chunk), BF16),
            pltpu.VMEM((n_all, chunk, rank), BF16),
            pltpu.VMEM((feats, cols), F32),
            pltpu.VMEM((feats, cols), BF16),
            pltpu.VMEM((feats, cols), BF16),
            pltpu.VMEM((docs, slots), BF16),
            pltpu.VMEM((n_row * n_col * PAD, rank), F32),
            pltpu.VMEM((n_row * n_col * PAD, rank), F32),
            pltpu.VMEM((n_col, docs, rank), F32),
            pltpu.VMEM((n_col, docs, rank), BF16),
            pltpu.VMEM((n_col, docs, rank), BF16),
            pltpu.VMEM((ny, NZ, rows, cols), F32),
            pltpu.VMEM((CHUNKS, NZ - 1, NZ, rows, cols * max(WIDTHS) // sum(WIDTHS)), F32),
            pltpu.VMEM((CHUNKS, NZ, rows, cols * max(WIDTHS) // sum(WIDTHS)), F32),
            pltpu.VMEM((CHUNKS, NZ - 1, rows, cols * max(WIDTHS) // sum(WIDTHS)), F32),
            dma((n_all,)), dma((n_all,)), dma,
            dma, dma,
            dma((nx,)), dma((nx,)), dma((nx,)), dma((nx,)),
            dma((CHUNKS, NZ)), dma((CHUNKS, NZ)), dma((CHUNKS, NZ)), dma((CHUNKS, NZ)),
        ],
        compiler_params=pltpu.CompilerParams(
            collective_id=0, has_side_effects=True, vmem_limit_bytes=56 << 20
        ),
    )(
        saved_inputs, output_grads, proj_in, proj_out,
        doc_lengths.reshape(1, docs), device_docs.reshape(1, docs), fisher_inverse,
    )


def solution(mesh):
    placed = (P(("row", "col"), None), P(("row", "col"), None), P(), P(), P(), P(), P("row", "col"))
    return jax.shard_map(
        per_device, mesh=mesh, in_specs=placed, out_specs=P("row", "col"), check_vma=False
    )
```

```python
import jax
import jax.numpy as jnp
from jax import lax
from jax.experimental import pallas as pl
from jax.experimental.pallas import tpu as pltpu
from jax.sharding import PartitionSpec as P

SLOTS = 5
PAD = 8
CORES = 2
NZ = 4
WIDTHS = (1, 1, 2, 2, 1, 1)
CHUNKS = len(WIDTHS)
EARLY = 2
F32 = jnp.float32
BF16 = jnp.bfloat16
MESH = pl.DeviceIdType.MESH


def split(x):
    hi = x.astype(BF16)
    return hi, (x - hi.astype(F32)).astype(BF16)


def dot(a, b):
    return jnp.dot(a, b, preferred_element_type=F32)


def body(
    chunk, si, og, pi, po, dl, dd, fi, out,
    x, w, f32buf, fhi, flo, sel, pbuf, tbuf, gbuf, ghi, glo, ybuf, mbuf, qbuf, obuf,
    x_sem, w_sem, f_sem, s1, r1, s3, r3, s5, r5, s4, r4, s6, r6,
):
    n_row = lax.axis_size("row")
    n_col = lax.axis_size("col")
    row = lax.axis_index("row")
    col = lax.axis_index("col")
    tok, d_in = si.shape
    rank = pi.shape[1]
    docs = dl.shape[1]
    n_in = d_in // chunk
    n_all = n_in + og.shape[1] // chunk
    n_dev = n_row * n_col
    me = row * n_col + col

    def each_other(act):
        for lo, hi in ((n_row // 2, n_row), (1, n_row // 2)):
            @pl.loop(lo, hi)
            def _(j):
                to = lax.rem(row + j, n_row)
                for c in range(n_col):
                    act(to, c)

        @pl.loop(1, n_col)
        def _(j):
            act(row, lax.rem(col + j, n_col))

    loads = []
    for k in range(n_all):
        a, b, i = (si, pi, k) if k < n_in else (og, po, k - n_in)
        cols = pl.ds(i * chunk, chunk)
        loads.append((
            pltpu.make_async_copy(a.at[:, cols], x.at[k], x_sem.at[k]),
            pltpu.make_async_copy(b.at[cols, :], w.at[k], w_sem.at[k]),
        ))
        for c in loads[-1]:
            c.start()
    f_load = pltpu.make_async_copy(fi, f32buf, f_sem)

    barrier = pltpu.get_barrier_semaphore()

    def greet(to_row, to_col):
        pl.semaphore_signal(barrier, inc=1, device_id={"row": to_row, "col": to_col}, device_id_type=MESH)

    each_other(greet)

    lens = jnp.broadcast_to(dl[...].astype(F32), (docs, docs))
    down = lax.broadcasted_iota(jnp.int32, (docs, docs), 0)
    along = lax.broadcasted_iota(jnp.int32, (docs, docs), 1)
    starts_col = jnp.sum(jnp.where(along < down, lens, 0.0), axis=1, keepdims=True)
    starts_row = jnp.sum(jnp.where(down == along, starts_col, 0.0), axis=0, keepdims=True)

    base = me * tok
    pos = base + lax.broadcasted_iota(jnp.int32, (tok, 1), 0)
    begun = (starts_row <= pos.astype(F32)) & (starts_row > jnp.full((1, 1), base, jnp.int32).astype(F32))
    slot = jnp.sum(jnp.where(begun, 1.0, 0.0), axis=1, keepdims=True)

    low = []
    for lo, hi in ((0, n_in), (n_in, n_all)):
        acc = None
        for k in range(lo, hi):
            for c in loads[k]:
                c.wait()
            term = dot(x[k], w[k])
            acc = term if acc is None else acc + term
        low.append(acc.astype(BF16))
    low_in, low_out = low
    masked = jnp.concatenate(
        [jnp.where(slot == float(s), low_in, jnp.zeros_like(low_in)) for s in range(SLOTS)], axis=1
    )
    part = lax.dot_general(low_out, masked, (((0,), (0,)), ((), ())), preferred_element_type=F32)
    for s in range(SLOTS):
        pbuf[pl.ds(s, rank, stride=PAD), :] = part[:, s * rank:(s + 1) * rank]

    pl.semaphore_wait(barrier, n_dev - 1)

    def slots_of(ref, i):
        return ref.at[pl.ds(pl.multiple_of(i * PAD, PAD), SLOTS), :]

    def give(to_row, to_col):
        pltpu.make_async_remote_copy(
            src_ref=slots_of(pbuf, to_row * n_col + to_col), dst_ref=slots_of(tbuf, me), send_sem=s1, recv_sem=r1,
            device_id={"row": to_row, "col": to_col}, device_id_type=MESH,
        ).start()

    f_load.start()
    each_other(give)

    at = pl.ds(pl.multiple_of(me * PAD, PAD), SLOTS)
    tbuf[at, :] = pbuf[at, :]

    owner_col = jnp.sum(jnp.where(down == along, dd[...].astype(F32), 0.0), axis=1, keepdims=True)

    lanes = lax.broadcasted_iota(jnp.int32, (1, SLOTS * n_dev), 1)
    first = jnp.sum(jnp.where(starts_col <= (lax.rem(lanes, n_dev) * tok).astype(F32), 1.0, 0.0), axis=0, keepdims=True) - 1.0
    slot_doc = first + (lanes // n_dev).astype(F32)
    sel[...] = jnp.where(owner_col == slot_doc, 1.0, 0.0).astype(BF16)

    f_load.wait()

    @pl.loop(0, fi.shape[0] // 32)
    def _(i):
        at = pl.ds(pl.multiple_of(i * 32, 32), 32)
        fhi[at, :], flo[at, :] = split(f32buf[at, :])

    others = pl.ds(0, (n_dev - 1) * SLOTS)
    pltpu.make_async_copy(tbuf.at[others, :], tbuf.at[others, :], r1).wait()

    t_hi, t_lo = split(jnp.concatenate([tbuf[pl.ds(s, n_dev, stride=PAD), :] for s in range(SLOTS)], axis=0))
    gbuf[col] = dot(sel[...], t_hi) + dot(sel[...], t_lo)

    nx = n_col // CORES
    cx = col // CORES
    core = lax.rem(col, CORES)
    sibling = col + 1 - 2 * core

    def hand(at, to, send, recv):
        return pltpu.make_async_remote_copy(
            src_ref=gbuf.at[at], dst_ref=gbuf.at[at], send_sem=send, recv_sem=recv,
            device_id={"row": row, "col": to}, device_id_type=MESH,
        )

    def keep(at):
        ghi[at], glo[at] = split(gbuf[at])

    around = [hand(col, lax.rem(cx + j, nx) * CORES + core, s3.at[j], r3.at[j]) for j in range(1, nx)]
    across = [hand(col, sibling, s5.at[0], r5.at[0])]
    for c in around + across:
        c.start()
    keep(col)
    for j in range(1, nx):
        around[j - 1].wait_recv()
        at = lax.rem(cx + nx - j, nx) * CORES + core
        across.append(hand(at, sibling, s5.at[j], r5.at[j]))
        across[j].start()
        keep(at)
    def product(side, cols):
        at = [x * CORES + side for x in range(nx)]
        a_hi, a_lo = (jnp.concatenate([b[c] for c in at], axis=1) for b in (ghi, glo))
        b_hi, b_lo = (
            jnp.concatenate([b[pl.ds(pl.multiple_of(c * rank, rank), rank), cols] for c in at], axis=0) for b in (fhi, flo)
        )
        return dot(a_hi, b_hi) + (dot(a_hi, b_lo) + dot(a_lo, b_hi))

    unit = ybuf.shape[3] // sum(WIDTHS)
    begin = [unit * sum(WIDTHS[:n]) for n in range(CHUNKS + 1)]
    for n in range(EARLY):
        cols = slice(begin[n], begin[n + 1])
        ybuf[:, :, :, cols] = product(core, cols).reshape(n_row // NZ, NZ, docs // n_row, begin[n + 1] - begin[n])
    for j in range(nx):
        across[j].wait_recv()
        keep(lax.rem(cx + nx - j, nx) * CORES + 1 - core)

    ny = n_row // NZ
    y, z = row // NZ, lax.rem(row, NZ)
    rows = docs // n_row
    g_hi = jnp.concatenate([ghi[c] for c in range(n_col)], axis=1)
    g_lo = jnp.concatenate([glo[c] for c in range(n_col)], axis=1)

    def peer(along_y, j):
        if along_y:
            to = lax.rem(y + j, ny)
            return to, {"row": to * NZ + z, "col": col}
        to = lax.rem(z + j, NZ)
        return to, {"row": y * NZ + to, "col": col}

    first_hop, second_hop = [], []
    for n in range(CHUNKS):
        cols = slice(begin[n], begin[n + 1])
        wide = begin[n + 1] - begin[n]
        if n < EARLY:
            ybuf[:, :, :, cols] += product(1 - core, cols).reshape(ny, NZ, rows, wide)
        else:
            f_hi, f_lo = fhi[:, cols], flo[:, cols]
            prod = dot(g_hi, f_hi) + (dot(g_hi, f_lo) + dot(g_lo, f_hi))
            ybuf[:, :, :, cols] = prod.reshape(ny, NZ, rows, wide)
        hops = []
        for j in range(1, ny if n % 2 == 0 else NZ):
            to, device = peer(n % 2 == 0, j)
            src = ybuf.at[to, :, :, cols] if n % 2 == 0 else ybuf.at[:, to, :, cols]
            hops.append(pltpu.make_async_remote_copy(
                src_ref=src, dst_ref=mbuf.at[n, j - 1, :, :, 0:wide], send_sem=s4.at[n, j], recv_sem=r4.at[n, j],
                device_id=device, device_id_type=MESH,
            ))
            hops[-1].start()
        first_hop.append(hops)

    for n in range(CHUNKS):
        cols = slice(begin[n], begin[n + 1])
        wide = begin[n + 1] - begin[n]
        part = ybuf[y, :, :, cols] if n % 2 == 0 else ybuf[:, z, :, cols]
        for j, c in enumerate(first_hop[n]):
            c.wait_recv()
            part = part + mbuf[n, j, :, :, 0:wide]
        qbuf[n, :, :, 0:wide] = part
        hops = []
        for j in range(1, NZ if n % 2 == 0 else ny):
            to, device = peer(n % 2 == 1, j)
            hops.append(pltpu.make_async_remote_copy(
                src_ref=qbuf.at[n, to, :, 0:wide], dst_ref=obuf.at[n, j - 1, :, 0:wide], send_sem=s6.at[n, j], recv_sem=r6.at[n, j],
                device_id=device, device_id_type=MESH,
            ))
            hops[-1].start()
        second_hop.append(hops)

    for n in range(CHUNKS):
        wide = begin[n + 1] - begin[n]
        total = qbuf[n, z if n % 2 == 0 else y, :, 0:wide]
        for j, c in enumerate(second_hop[n]):
            c.wait_recv()
            total = total + obuf[n, j, :, 0:wide]
        out[:, begin[n]:begin[n + 1]] = total

    pltpu.make_async_copy(pbuf.at[others, :], pbuf.at[others, :], s1).wait()
    for c in around + across + sum(first_hop + second_hop, []):
        c.wait_send()


def per_device(saved_inputs, output_grads, proj_in, proj_out, doc_lengths, device_docs, fisher_inverse):
    n_row, n_col = lax.axis_size("row"), lax.axis_size("col")
    tok, d_in = saved_inputs.shape
    ff = output_grads.shape[1]
    rank = proj_in.shape[1]
    docs = doc_lengths.shape[0]
    feats, cols = fisher_inverse.shape
    chunk = 2048
    n_all = (d_in + ff) // chunk
    slots = n_row * n_col * SLOTS
    ny, nx, rows = n_row // NZ, n_col // CORES, docs // n_row
    dma = pltpu.SemaphoreType.DMA
    hbm = pl.BlockSpec(memory_space=pl.ANY)
    vmem = pl.BlockSpec(memory_space=pltpu.VMEM)

    def kernel(*refs):
        body(chunk, *refs)

    return pl.pallas_call(
        kernel,
        out_shape=pltpu.VMEM((docs // n_row, cols), F32),
        in_specs=[hbm, hbm, hbm, hbm, vmem, vmem, hbm],
        out_specs=vmem,
        scratch_shapes=[
            pltpu.VMEM((n_all, tok, chunk), BF16),
            pltpu.VMEM((n_all, chunk, rank), BF16),
            pltpu.VMEM((feats, cols), F32),
            pltpu.VMEM((feats, cols), BF16),
            pltpu.VMEM((feats, cols), BF16),
            pltpu.VMEM((docs, slots), BF16),
            pltpu.VMEM((n_row * n_col * PAD, rank), F32),
            pltpu.VMEM((n_row * n_col * PAD, rank), F32),
            pltpu.VMEM((n_col, docs, rank), F32),
            pltpu.VMEM((n_col, docs, rank), BF16),
            pltpu.VMEM((n_col, docs, rank), BF16),
            pltpu.VMEM((ny, NZ, rows, cols), F32),
            pltpu.VMEM((CHUNKS, NZ - 1, NZ, rows, cols * max(WIDTHS) // sum(WIDTHS)), F32),
            pltpu.VMEM((CHUNKS, NZ, rows, cols * max(WIDTHS) // sum(WIDTHS)), F32),
            pltpu.VMEM((CHUNKS, NZ - 1, rows, cols * max(WIDTHS) // sum(WIDTHS)), F32),
            dma((n_all,)), dma((n_all,)), dma,
            dma, dma,
            dma((nx,)), dma((nx,)), dma((nx,)), dma((nx,)),
            dma((CHUNKS, NZ)), dma((CHUNKS, NZ)), dma((CHUNKS, NZ)), dma((CHUNKS, NZ)),
        ],
        compiler_params=pltpu.CompilerParams(
            collective_id=0, has_side_effects=True, vmem_limit_bytes=56 << 20
        ),
    )(
        saved_inputs, output_grads, proj_in, proj_out,
        doc_lengths.reshape(1, docs), device_docs.reshape(1, docs), fisher_inverse,
    )


def solution(mesh):
    placed = (P(("row", "col"), None), P(("row", "col"), None), P(), P(), P(), P(), P("row", "col"))
    return jax.shard_map(
        per_device, mesh=mesh, in_specs=placed, out_specs=P("row", "col"), check_vma=False
    )
```
